512 devices in a mesh: row: 16 (over z, core), col: 32 (over x, y).
Axes of the slice: x: 4, y: 8, z: 8, core: 2. Of those that a mesh axis runs over, the one named last changes fastest.
Arguments:
- panel: bfloat16 [64, 1024, 256], P('row', 'col'), may hold values from -6 to 6
- inverse_factor: bfloat16 [1024, 1024], P('row', 'col'), as said below
- ranks: int32 [64], replicated, may hold values from 32 to 256
Outputs:
- solved: bfloat16 [64, 1024, 256], P('row', 'col')
- core_blocks: bfloat16 [64, 64, 256, 256], P('row', 'col')
The draws below stay inside these ranges and needn't reach their ends.
Inputs may be any that keep to these rules, and one draw needn't show every extreme that they name: inverse_factor is lower triangular with a diagonal between 0.5 and 3.
All inputs are finite; a program needn't handle non-finite values.
Results may differ from the reference program's by a relative error of at most 0.017.
Values may be sent and summed in bfloat16 or wider, within the bound.
No kernel may reach another device: no remote copies, remote signals or barrier semaphores. Data moves between devices by JAX's collectives and lax.ppermute only.
A program may use at most 64 MiB of HBM per device.

```python
import math
import jax
import jax.numpy as jnp
from jax import lax

NB = 1024
RMAX = 256
TILES = 64
N_COL = 32


def draw_inverse_factor(key, part):
    key_lower = jax.random.fold_in(key, 11)
    key_diag = jax.random.fold_in(key, 12)
    lower_part = jax.random.normal(key_lower, (NB, NB), jnp.float32) * (1.0 / math.sqrt(NB))
    diagonal = jax.random.uniform(key_diag, (NB,), jnp.float32, minval=0.5, maxval=1.5)
    positions = jnp.arange(NB)
    matrix = jnp.where(positions[:, None] > positions[None, :], lower_part, 0.0) + jnp.diag(diagonal)
    return matrix.astype(jnp.bfloat16)


def place_ends(values, rng, smallest, high):
    longest = values.shape.index(max(values.shape))
    spots = []
    for shift in (0, 1):
        where = [jax.random.randint(jax.random.fold_in(rng, axis), (), 0, length) for axis, length in enumerate(values.shape)]
        where[longest] = (where[longest] + shift) % values.shape[longest]
        spots.append(tuple(where))
    return values.at[spots[0]].set(smallest).at[spots[1]].set(high)


def block_levels(key, dims, split, low, top_value):
    def one(dim, blocks):
        steps = jax.random.uniform(jax.random.fold_in(jax.random.fold_in(key, 6), dim), (blocks,), jnp.float32, low / len(split), top_value / len(split))
        return jnp.repeat(jnp.exp(steps), dims[dim] // blocks).reshape((-1,) + (1,) * (len(dims) - dim - 1))

    level = one(*split[0])
    for cut in split[1:]:
        level = level * one(*cut)
    return level


def gaussian(key, shape, width, limit, split=(), held_as=jnp.bfloat16):
    level = block_levels(key, shape, split, -0.22, 0.18) if split else 1.0
    entries = jax.random.normal(key, shape, jnp.float32) * width * level
    return jnp.minimum(jnp.maximum(entries, -limit), limit).astype(held_as)


def setup_inputs(seed: int = 0) -> dict:
    key_of = jax.random.split(jax.random.key(seed), 4)
    return {
        "panel": gaussian(key_of[0], (TILES, NB, RMAX), 1.0, 6.0, ((0, 16), (1, 32))),
        "inverse_factor": draw_inverse_factor(jax.random.fold_in(key_of[3], 71), 0),
        "ranks": place_ends(jax.random.randint(key_of[2], (TILES,), RMAX // 8, RMAX + 1), jax.random.fold_in(key_of[2], 1), RMAX // 8, RMAX).astype(jnp.int32),
    }


def reference(panel, inverse_factor, ranks):
    column_ids = jnp.arange(RMAX, dtype=jnp.int32)
    keep_cols = (column_ids[None, :] < ranks[:, None]).astype(jnp.bfloat16)
    masked = panel * keep_cols[:, None, :]
    slice_width = NB // N_COL

    def add_block(block_index, running):
        first = (block_index * slice_width).astype(jnp.int32)
        factor_part = lax.dynamic_slice_in_dim(inverse_factor, first, slice_width, 1).astype(jnp.float32)
        panel_part = lax.dynamic_slice_in_dim(masked, first, slice_width, 1).astype(jnp.float32)
        product = jnp.einsum('ab,tbr->tar', factor_part, panel_part, precision=lax.Precision.HIGHEST)
        rounded = lax.optimization_barrier(product.astype(jnp.bfloat16))
        return running + rounded.astype(jnp.float32)

    running = lax.fori_loop(0, N_COL, add_block, jnp.zeros((TILES, NB, RMAX), jnp.float32))
    solved = running.astype(jnp.bfloat16)
    solved_wide = solved.astype(jnp.float32)

    def pair_row(left):
        return jnp.einsum('ar,uas->urs', left, solved_wide, precision=lax.Precision.HIGHEST).astype(jnp.bfloat16)

    core_blocks = lax.map(pair_row, solved_wide)
    return solved, core_blocks
```

```python
import jax
import jax.numpy as jnp
from jax import lax
from jax.sharding import Mesh
from jax.sharding import PartitionSpec as P

ROW = ("z", "core")
COL = ("x", "y")
ALL = ROW + COL


def size_of(axes):
    axes = axes if isinstance(axes, tuple) else (axes,)
    count = 1
    for axis in axes:
        count *= lax.axis_size(axis)
    return count


def sent_to_all(value, axes):
    copies = jnp.broadcast_to(value, (size_of(axes), *value.shape))
    return lax.all_to_all(copies, axes, split_axis=0, concat_axis=0, tiled=True)


def kept(value, ranks):
    columns = jnp.arange(value.shape[-1], dtype=jnp.int32)
    return value * (columns[None, :] < ranks[:, None]).astype(value.dtype)[:, None, :]


def column_tiles(panel, col, rows, cols):
    odd = lax.rem(col, 2)
    pair = panel.shape[0] // 2

    def moved(flip):
        half = lax.bitwise_xor(odd, flip)
        part = lax.dynamic_slice_in_dim(panel, pair * half, pair, 0)
        pairs = [
            (r * cols + c, (c // 2) * cols + 2 * r + ((c % 2) ^ flip))
            for r in range(rows)
            for c in range(cols)
        ]
        return lax.ppermute(part, ALL, pairs)

    first, second = moved(0), moved(1)
    low = jnp.where(odd == 0, first, second)
    high = jnp.where(odd == 0, second, first)
    return jnp.concatenate([low, high], axis=1)


def per_device(panel, inverse_factor, ranks):
    tiles, depth, width = panel.shape
    core = lax.axis_index("core")
    row = lax.axis_index(ROW)
    col = lax.axis_index(COL)
    rows, cols = size_of(ROW), size_of(COL)
    pair = tiles * rows // cols

    part = column_tiles(panel, col, rows, cols)

    factor = lax.all_gather(inverse_factor.T, "core", axis=1, tiled=True)
    half = depth // 2
    lanes = factor.shape[1]
    factor = lax.dynamic_slice_in_dim(factor, half * core, half, 0)
    factor = sent_to_all(factor, COL)

    part_rows = part.shape[1]
    sides = width // lanes
    packed = jnp.concatenate(
        [
            factor.reshape(cols * half, lanes),
            jnp.moveaxis(part.reshape(pair, part_rows, sides, lanes), 2, 0).reshape(-1, lanes),
        ],
        axis=0,
    )
    packed = lax.all_gather(packed, ROW)
    count = cols * half
    whole = packed[:, :count].reshape(rows // 2, 2, cols, half, lanes)
    whole = whole.transpose(2, 1, 3, 0, 4).reshape(cols * depth, -1)
    mine = packed[:, count:].reshape(rows, sides, pair, part_rows, lanes)
    mine = mine.transpose(2, 0, 3, 1, 4).reshape(pair, rows * part_rows, width)

    full = sent_to_all(sent_to_all(panel, "y"), "x")
    full = full.reshape(cols, tiles, depth, width).transpose(1, 0, 2, 3)
    full = full.reshape(tiles, cols * depth, width)

    full = kept(full, lax.dynamic_slice_in_dim(ranks, row * tiles, tiles, 0))
    mine = kept(mine, lax.dynamic_slice_in_dim(ranks, col * pair, pair, 0))

    def solve(value):
        out = jnp.einsum("ba,tbr->tar", whole, value, preferred_element_type=jnp.float32)
        return out.astype(jnp.bfloat16)

    solved_full = solve(full)
    solved_mine = solve(mine)
    shares = lax.dynamic_slice_in_dim(solved_full, col * depth, depth, 1)
    core_blocks = jnp.einsum(
        "tar,uas->turs", solved_full, solved_mine, preferred_element_type=jnp.float32
    ).astype(jnp.bfloat16)
    return shares, core_blocks


def solution(mesh):
    split = Mesh(mesh.devices.reshape(8, 2, 4, 8), ALL)
    return jax.shard_map(
        per_device,
        mesh=split,
        in_specs=(P(ROW, COL, None), P(ROW, COL), P()),
        out_specs=(P(ROW, COL, None), P(ROW, COL, None, None)),
        check_vma=False,
    )
```

```python
import jax
import jax.numpy as jnp
from jax import lax
from jax.experimental import pallas as pl
from jax.experimental.pallas import tpu as pltpu
from jax.sharding import Mesh
from jax.sharding import PartitionSpec as P

ROW = ("z", "core")
COL = ("x", "y")
ALL = ROW + COL


def size_of(axes):
    axes = axes if isinstance(axes, tuple) else (axes,)
    count = 1
    for axis in axes:
        count *= lax.axis_size(axis)
    return count


def sent_to_all(value, axes):
    copies = jnp.broadcast_to(value, (size_of(axes), *value.shape))
    return lax.all_to_all(copies, axes, split_axis=0, concat_axis=0, tiled=True)


def column_tiles(panel, col, rows, cols):
    odd = lax.rem(col, 2)
    pair = panel.shape[0] // 2

    def moved(flip):
        half = lax.bitwise_xor(odd, flip)
        part = lax.dynamic_slice_in_dim(panel, pair * half, pair, 0)
        pairs = [
            (r * cols + c, (c // 2) * cols + 2 * r + ((c % 2) ^ flip))
            for r in range(rows)
            for c in range(cols)
        ]
        return lax.ppermute(part, ALL, pairs)

    first, second = moved(0), moved(1)
    low = jnp.where(odd == 0, first, second)
    high = jnp.where(odd == 0, second, first)
    return jnp.concatenate([low, high], axis=1)


LANES = 128
STEP = 2 * LANES


def solve_and_pair(ranks, packed, full, shares, core_blocks, values, factor, solved):
    cols, tiles, depth, width = full.shape
    rows = packed.shape[0]
    pair = core_blocks.shape[1]
    half = depth // 2
    steps = cols * depth // STEP
    group = cols // steps
    count = cols * half
    row = lax.axis_index(ROW)
    col = lax.axis_index(COL)
    lane = lax.broadcasted_iota(jnp.int32, (1, 1, width), 2)

    for z in range(rows // 2):
        for k in range(2):
            for g in range(steps):
                factor[pl.ds(LANES * z, LANES), pl.ds(STEP * g + LANES * k, LANES)] = packed[
                    2 * z + k, pl.ds(LANES * g, LANES), :
                ]

    def fill_own(t, carry):
        keep = (lane < ranks[row * tiles + t]).astype(jnp.bfloat16)
        for k in range(2):
            part = full[:, t, pl.ds(half * k, half), :] * keep
            for g in range(steps):
                values[t, pl.ds(STEP * g + LANES * k, LANES), :] = part[
                    group * g : group * (g + 1)
                ].reshape(LANES, width)
        return carry

    lax.fori_loop(0, tiles, fill_own, 0)

    part_rows = 2 * depth
    for u in range(pair):
        for h in range(width // LANES):
            keep = (lane[:, :, LANES * h : LANES * (h + 1)] < ranks[col * pair + u]).astype(
                jnp.bfloat16
            )
            start = count + (h * pair + u) * part_rows
            part = (packed[:, pl.ds(start, part_rows), :] * keep).reshape(cols, depth, LANES)
            for k in range(2):
                piece = part[:, half * k : half * (k + 1), :]
                for g in range(steps):
                    values[
                        tiles + u,
                        pl.ds(STEP * g + LANES * k, LANES),
                        pl.ds(LANES * h, LANES),
                    ] = piece[group * g : group * (g + 1)].reshape(LANES, LANES)

    def solve(t, carry):
        for i in range(steps):
            known = STEP * (i + 1)
            block = pl.ds(STEP * i, STEP)
            solved[t, block, :] = jnp.dot(
                factor[block, :known], values[t, :known, :], preferred_element_type=jnp.float32
            ).astype(jnp.bfloat16)
        return carry

    lax.fori_loop(0, tiles + pair, solve, 0)
    first = pl.multiple_of(col * depth, depth)
    for t in range(tiles):
        shares[t] = solved[t, pl.ds(first, depth), :]

    def blocks(t, carry):
        for u in range(pair):
            core_blocks[t, u] = lax.dot_general(
                solved[t],
                solved[tiles + u],
                (((0,), (0,)), ((), ())),
                preferred_element_type=jnp.float32,
            ).astype(jnp.bfloat16)
        return carry

    lax.fori_loop(0, tiles, blocks, 0)


def finish(ranks, packed, full, pair):
    cols, tiles, depth, width = full.shape
    in_vmem = pl.BlockSpec(memory_space=pltpu.VMEM)
    height = cols * depth
    return pl.pallas_call(
        solve_and_pair,
        out_shape=(
            jax.ShapeDtypeStruct((tiles, depth, width), jnp.bfloat16),
            jax.ShapeDtypeStruct((tiles, pair, width, width), jnp.bfloat16),
        ),
        in_specs=[pl.BlockSpec(memory_space=pltpu.SMEM), in_vmem, in_vmem],
        out_specs=(in_vmem, in_vmem),
        scratch_shapes=[
            pltpu.VMEM((tiles + pair, height, width), jnp.bfloat16),
            pltpu.VMEM((height, height), jnp.bfloat16),
            pltpu.VMEM((tiles + pair, height, width), jnp.bfloat16),
        ],
        compiler_params=pltpu.CompilerParams(vmem_limit_bytes=40 << 20),
        cost_estimate=pl.CostEstimate(
            flops=2 * height * height * width * (tiles + pair), bytes_accessed=8 << 20, transcendentals=0
        ),
    )(ranks, packed, full)


def per_device(panel, inverse_factor, ranks):
    tiles, depth, width = panel.shape
    core = lax.axis_index("core")
    col = lax.axis_index(COL)
    rows, cols = size_of(ROW), size_of(COL)
    pair = tiles * rows // cols

    part = column_tiles(panel, col, rows, cols)

    factor = lax.all_gather(inverse_factor.T, "core", axis=1, tiled=True)
    half = depth // 2
    factor = lax.dynamic_slice_in_dim(factor, half * core, half, 0)
    factor = sent_to_all(factor, COL).reshape(-1, LANES, LANES)
    factor = factor.transpose(0, 2, 1).reshape(-1, LANES)

    sides = width // LANES
    side_parts = [part[:, :, LANES * h : LANES * (h + 1)].reshape(-1, LANES) for h in range(sides)]
    packed = lax.all_gather(jnp.concatenate([factor, *side_parts], axis=0), ROW)

    full = sent_to_all(sent_to_all(panel, "y"), "x").reshape(cols, tiles, depth, width)
    return finish(ranks, packed, full, pair)


def solution(mesh):
    split = Mesh(mesh.devices.reshape(8, 2, 4, 8), ALL)
    return jax.shard_map(
        per_device,
        mesh=split,
        in_specs=(P(ROW, COL, None), P(ROW, COL), P()),
        out_specs=(P(ROW, COL, None), P(ROW, COL, None, None)),
        check_vma=False,
    )
```

```python
import jax
import jax.numpy as jnp
from jax import lax
from jax.experimental import pallas as pl
from jax.experimental.pallas import tpu as pltpu
from jax.sharding import Mesh
from jax.sharding import PartitionSpec as P

ROW = ("z", "core")
COL = ("x", "y")
ALL = ROW + COL


def size_of(axes):
    axes = axes if isinstance(axes, tuple) else (axes,)
    count = 1
    for axis in axes:
        count *= lax.axis_size(axis)
    return count


def sent_to_all(value, axes):
    copies = jnp.broadcast_to(value, (size_of(axes), *value.shape))
    return lax.all_to_all(copies, axes, split_axis=0, concat_axis=0, tiled=True)


def column_tiles(panel, col, rows, cols):
    odd = lax.rem(col, 2)
    pair = panel.shape[0] // 2

    def moved(flip):
        half = lax.bitwise_xor(odd, flip)
        part = lax.dynamic_slice_in_dim(panel, pair * half, pair, 0)
        pairs = [
            (r * cols + c, (c // 2) * cols + 2 * r + ((c % 2) ^ flip))
            for r in range(rows)
            for c in range(cols)
        ]
        return lax.ppermute(part, ALL, pairs)

    first, second = moved(0), moved(1)
    low = jnp.where(odd == 0, first, second)
    high = jnp.where(odd == 0, second, first)
    return jnp.concatenate([low, high], axis=1)


LANES = 128
STEP = 2 * LANES
NEAR = (0, 2, 6, 4)
ODD = (1, 3, 7, 5)


def solve_and_pair(ranks, here, there, full, shares, core_blocks, values, factor, solved):
    cols, tiles, depth, width = full.shape
    pair = core_blocks.shape[1]
    half = depth // 2
    steps = cols * depth // STEP
    group = cols // steps
    count = cols * half
    row = lax.axis_index(ROW)
    col = lax.axis_index(COL)
    level = lax.axis_index("z")
    core = lax.axis_index("core")
    levels = lax.axis_size("z")
    lane = lax.broadcasted_iota(jnp.int32, (1, 1, width), 2)
    part_rows = 2 * depth

    keeps = [
        [
            (lane[0, :, LANES * h : LANES * (h + 1)] < ranks[col * pair + u]).astype(jnp.bfloat16)
            for h in range(width // LANES)
        ]
        for u in range(pair)
    ]
    for source, k in ((here, core), (there, 1 - core)):
        for n, shift in enumerate(NEAR + ODD):
            z = lax.rem(level + shift, levels)
            top = pl.multiple_of(LANES * z, LANES)
            for g in range(steps):
                left = pl.multiple_of(STEP * g + LANES * k, LANES)
                factor[pl.ds(top, LANES), pl.ds(left, LANES)] = source[n, pl.ds(LANES * g, LANES), :]
            place = STEP * (z // 2) + half * (4 * lax.rem(z, 2) + 2 * k)
            for u in range(pair):
                for h in range(width // LANES):
                    start = count + (h * pair + u) * part_rows
                    part = source[n, pl.ds(start, part_rows), :] * keeps[u][h]
                    for q in range(2):
                        for side in range(2):
                            first = pl.multiple_of(place + half * q + LANES * side, half)
                            values[tiles + u, pl.ds(first, half), pl.ds(LANES * h, LANES)] = part[
                                half * (2 * q + side) : half * (2 * q + side + 1)
                            ]

    def fill_own(t, carry):
        keep = (lane < ranks[row * tiles + t]).astype(jnp.bfloat16)
        for k in range(2):
            part = full[:, t, pl.ds(half * k, half), :] * keep
            for g in range(steps):
                values[t, pl.ds(STEP * g + LANES * k, LANES), :] = part[
                    group * g : group * (g + 1)
                ].reshape(LANES, width)
        return carry

    lax.fori_loop(0, tiles, fill_own, 0)

    def solve(t, carry):
        for i in range(steps):
            known = STEP * (i + 1)
            block = pl.ds(STEP * i, STEP)
            solved[t, block, :] = jnp.dot(
                factor[block, :known], values[t, :known, :], preferred_element_type=jnp.float32
            ).astype(jnp.bfloat16)
        return carry

    lax.fori_loop(0, tiles + pair, solve, 0)
    first = pl.multiple_of(col * depth, depth)
    for t in range(tiles):
        shares[t] = solved[t, pl.ds(first, depth), :]

    def blocks(t, carry):
        for u in range(pair):
            core_blocks[t, u] = lax.dot_general(
                solved[t],
                solved[tiles + u],
                (((0,), (0,)), ((), ())),
                preferred_element_type=jnp.float32,
            ).astype(jnp.bfloat16)
        return carry

    lax.fori_loop(0, tiles, blocks, 0)


def finish(ranks, here, there, full, pair):
    cols, tiles, depth, width = full.shape
    in_vmem = pl.BlockSpec(memory_space=pltpu.VMEM)
    height = cols * depth
    return pl.pallas_call(
        solve_and_pair,
        out_shape=(
            jax.ShapeDtypeStruct((tiles, depth, width), jnp.bfloat16),
            jax.ShapeDtypeStruct((tiles, pair, width, width), jnp.bfloat16),
        ),
        in_specs=[pl.BlockSpec(memory_space=pltpu.SMEM), in_vmem, in_vmem, in_vmem],
        out_specs=(in_vmem, in_vmem),
        scratch_shapes=[
            pltpu.VMEM((tiles + pair, height, width), jnp.bfloat16),
            pltpu.VMEM((height, height), jnp.bfloat16),
            pltpu.VMEM((tiles + pair, height, width), jnp.bfloat16),
        ],
        compiler_params=pltpu.CompilerParams(vmem_limit_bytes=20 << 20),
        cost_estimate=pl.CostEstimate(
            flops=2 * height * height * width * (tiles + pair), bytes_accessed=8 << 20, transcendentals=0
        ),
    )(ranks, here, there, full)


def from_level(value, shift):
    levels = lax.axis_size("z")
    return lax.ppermute(value, "z", [((z + shift) % levels, z) for z in range(levels)])


def per_device(panel, inverse_factor, ranks):
    tiles, depth, width = panel.shape
    core = lax.axis_index("core")
    col = lax.axis_index(COL)
    rows, cols = size_of(ROW), size_of(COL)
    pair = tiles * rows // cols

    part = column_tiles(panel, col, rows, cols)

    factor = lax.all_gather(inverse_factor.T, "core", axis=1, tiled=True)
    half = depth // 2
    factor = lax.dynamic_slice_in_dim(factor, half * core, half, 0)
    factor = sent_to_all(factor, COL)
    factor, part, panel = lax.optimization_barrier((factor, part, panel))
    full = sent_to_all(panel, COL)

    factor = factor.reshape(-1, LANES, LANES).transpose(0, 2, 1).reshape(-1, LANES)
    sides = width // LANES
    side_parts = [part[:, :, LANES * h : LANES * (h + 1)].reshape(-1, LANES) for h in range(sides)]
    packed = jnp.concatenate([factor, *side_parts], axis=0)[None]

    opposite, above, below = from_level(packed, 4), from_level(packed, 2), from_level(packed, 6)
    upper = from_level(jnp.concatenate([packed, above]), 1)
    lower = from_level(jnp.concatenate([packed, below]), 7)
    here = jnp.concatenate([packed, above, below, opposite, upper, lower])
    there = lax.ppermute(here, "core", [(0, 1), (1, 0)])
    return finish(ranks, here, there, full, pair)


def solution(mesh):
    split = Mesh(mesh.devices.reshape(8, 2, 4, 8), ALL)
    return jax.shard_map(
        per_device,
        mesh=split,
        in_specs=(P(ROW, COL, None), P(ROW, COL), P()),
        out_specs=(P(ROW, COL, None), P(ROW, COL, None, None)),
        check_vma=False,
    )
```

```python
import jax
import jax.numpy as jnp
from jax import lax
from jax.experimental import pallas as pl
from jax.experimental.pallas import tpu as pltpu
from jax.sharding import Mesh
from jax.sharding import PartitionSpec as P


ROW = ("z", "core")
COL = ("x", "y")
ALL = ROW + COL


def size_of(axes):
    axes = axes if isinstance(axes, tuple) else (axes,)
    count = 1
    for axis in axes:
        count *= lax.axis_size(axis)
    return count


def copies_for(value, axes):
    return jnp.broadcast_to(value, (size_of(axes), *value.shape))


def exchanged(copies, axes):
    return lax.all_to_all(copies, axes, split_axis=0, concat_axis=0, tiled=True)


def column_tiles(panel, col, rows, cols):
    odd = lax.rem(col, 2)
    pair = panel.shape[0] // 2

    def moved(flip):
        half = lax.bitwise_xor(odd, flip)
        part = lax.dynamic_slice_in_dim(panel, pair * half, pair, 0)
        pairs = [
            (r * cols + c, (c // 2) * cols + 2 * r + ((c % 2) ^ flip))
            for r in range(rows)
            for c in range(cols)
        ]
        return lax.ppermute(part, ALL, pairs)

    first, second = moved(0), moved(1)
    low = jnp.where(odd == 0, first, second)
    high = jnp.where(odd == 0, second, first)
    return jnp.concatenate([low, high], axis=1)


NEAR = (0, 2, 6, 4)
ODD = (1, 3, 7, 5)
STEP = 256
IN_VMEM = pl.BlockSpec(memory_space=pltpu.VMEM)
IN_SMEM = pl.BlockSpec(memory_space=pltpu.SMEM)


def columns_kept(rank, width):
    lane = lax.broadcasted_iota(jnp.int32, (1, width), 1)
    return (lane < rank).astype(jnp.bfloat16)


def solve_block(factor, known_rows, keep, i):
    block = jnp.dot(
        factor[pl.ds(STEP * i, STEP), : STEP * (i + 1)],
        known_rows,
        preferred_element_type=jnp.float32,
    )
    return block.astype(jnp.bfloat16) * keep


def column_kernel(ranks, here, there, factor, solved, values):
    order = factor.shape[1]
    pair, _, width = solved.shape
    height = here.shape[1]
    col = lax.axis_index(COL)
    level = lax.axis_index("z")
    core = lax.axis_index("core")
    levels = lax.axis_size("z")
    for source, k in ((here, core), (there, 1 - core)):
        for n, shift in enumerate(NEAR + ODD):
            row = 2 * lax.rem(level + shift, levels) + k
            place = pl.ds(pl.multiple_of(height * row, height), height)
            factor[place, :] = source[n, :, :order]
            for u in range(pair):
                values[u, place, :] = source[n, :, order + width * u : order + width * (u + 1)]

    for u in range(pair):
        keep = columns_kept(ranks[col * pair + u], width)
        for i in range(order // STEP):
            solved[u, pl.ds(STEP * i, STEP), :] = solve_block(
                factor, values[u, : STEP * (i + 1), :], keep, i
            )


def solve_columns(ranks, here, there, pair, width, order):
    return pl.pallas_call(
        column_kernel,
        out_shape=(
            jax.ShapeDtypeStruct((order, order), jnp.bfloat16),
            jax.ShapeDtypeStruct((pair, order, width), jnp.bfloat16),
        ),
        in_specs=[IN_SMEM, IN_VMEM, IN_VMEM],
        out_specs=(IN_VMEM, IN_VMEM),
        scratch_shapes=[pltpu.VMEM((pair, order, width), jnp.bfloat16)],
        compiler_params=pltpu.CompilerParams(vmem_limit_bytes=16 << 20),
        cost_estimate=pl.CostEstimate(
            flops=2 * order * order * width * pair, bytes_accessed=6 << 20, transcendentals=0
        ),
    )(ranks, here, there)


def row_kernel(ranks, factor_in, others_in, full, shares, core_blocks, factor, others, solved, sems):
    _, tiles, depth, width = full.shape
    pair, order, _ = others.shape
    row = lax.axis_index(ROW)
    col = lax.axis_index(COL)
    steps = order // STEP

    def brought(i):
        if i == steps:
            return pltpu.make_async_copy(others_in, others, sems.at[i])
        block = pl.ds(STEP * i, STEP)
        return pltpu.make_async_copy(factor_in.at[block, :], factor.at[block, :], sems.at[i])

    for i in range(steps + 1):
        brought(i).start()

    def one(t, carry):
        keep = columns_kept(ranks[row * tiles + t], width)
        for i in range(steps):

            @pl.when(t == 0)
            def _():
                brought(i).wait()

            known = full[: STEP * (i + 1) // depth, t].reshape(STEP * (i + 1), width)
            solved[pl.ds(STEP * i, STEP), :] = solve_block(factor, known, keep, i)
        shares[t] = solved[pl.ds(pl.multiple_of(col * depth, depth), depth), :]

        @pl.when(t == 0)
        def _():
            brought(steps).wait()

        for u in range(pair):
            core_blocks[t, u] = lax.dot_general(
                solved[...],
                others[u],
                (((0,), (0,)), ((), ())),
                preferred_element_type=jnp.float32,
            ).astype(jnp.bfloat16)
        return carry

    lax.fori_loop(0, tiles, one, 0)


def solve_rows(ranks, factor, others, full):
    _, tiles, depth, width = full.shape
    pair, order, _ = others.shape
    in_hbm = pl.BlockSpec(memory_space=pltpu.HBM)
    return pl.pallas_call(
        row_kernel,
        out_shape=(
            jax.ShapeDtypeStruct((tiles, depth, width), jnp.bfloat16),
            jax.ShapeDtypeStruct((tiles, pair, width, width), jnp.bfloat16),
        ),
        in_specs=[IN_SMEM, in_hbm, in_hbm, IN_VMEM],
        out_specs=(IN_VMEM, IN_VMEM),
        scratch_shapes=[
            pltpu.VMEM((order, order), jnp.bfloat16),
            pltpu.VMEM((pair, order, width), jnp.bfloat16),
            pltpu.VMEM((order, width), jnp.bfloat16),
            pltpu.SemaphoreType.DMA((order // STEP + 1,)),
        ],
        compiler_params=pltpu.CompilerParams(vmem_limit_bytes=24 << 20),
        cost_estimate=pl.CostEstimate(
            flops=3 * order * order * width * tiles, bytes_accessed=6 << 20, transcendentals=0
        ),
    )(ranks, factor, others, full)


def from_level(value, shift):
    levels = lax.axis_size("z")
    return lax.ppermute(value, "z", [((z + shift) % levels, z) for z in range(levels)])


def per_device(panel, inverse_factor, ranks):
    tiles, depth, width = panel.shape
    col = lax.axis_index(COL)
    rows, cols = size_of(ROW), size_of(COL)
    pair = tiles * rows // cols
    order = cols * depth

    part = column_tiles(panel, col, rows, cols)
    factor = exchanged(copies_for(inverse_factor.T, COL), COL).reshape(order, -1).T

    packed = jnp.concatenate([factor, *part], axis=1)[None]
    copies, packed = lax.optimization_barrier((copies_for(panel, "y"), packed))
    along_y = exchanged(copies, "y")
    opposite, above, below = from_level(packed, 4), from_level(packed, 2), from_level(packed, 6)
    copies, opposite, above, below = lax.optimization_barrier(
        (copies_for(along_y, "x"), opposite, above, below)
    )
    full = exchanged(copies, "x")
    full = full.reshape(cols, tiles, depth, width)
    upper, lower = jnp.concatenate([packed, above]), jnp.concatenate([packed, below])
    upper = from_level(upper, 1)
    lower = from_level(lower, 7)
    here = jnp.concatenate([packed, above, below, opposite, upper, lower])
    there = lax.ppermute(here, "core", [(0, 1), (1, 0)])
    factor, others = solve_columns(ranks, here, there, pair, width, order)
    return solve_rows(ranks, factor, others, full)


def solution(mesh):
    split = Mesh(mesh.devices.reshape(8, 2, 4, 8), ALL)
    return jax.shard_map(
        per_device,
        mesh=split,
        in_specs=(P(ROW, COL, None), P(ROW, COL), P()),
        out_specs=(P(ROW, COL, None), P(ROW, COL, None, None)),
        check_vma=False,
    )
```

```python
import jax
import jax.numpy as jnp
from jax import lax
from jax.experimental import pallas as pl
from jax.experimental.pallas import tpu as pltpu
from jax.sharding import Mesh
from jax.sharding import PartitionSpec as P

ROW = ("z", "core")
COL = ("x", "y")
ALL = ROW + COL


def size_of(axes):
    axes = axes if isinstance(axes, tuple) else (axes,)
    count = 1
    for axis in axes:
        count *= lax.axis_size(axis)
    return count


def copies_for(value, axes):
    return jnp.broadcast_to(value, (size_of(axes), *value.shape))


def exchanged(copies, axes):
    return lax.all_to_all(copies, axes, split_axis=0, concat_axis=0, tiled=True)


def column_tiles(panel, col, rows, cols):
    odd = lax.rem(col, 2)
    pair = panel.shape[0] // 2

    def moved(flip):
        half = lax.bitwise_xor(odd, flip)
        part = lax.dynamic_slice_in_dim(panel, pair * half, pair, 0)
        pairs = [
            (r * cols + c, (c // 2) * cols + 2 * r + ((c % 2) ^ flip))
            for r in range(rows)
            for c in range(cols)
        ]
        return lax.ppermute(part, ALL, pairs)

    first, second = moved(0), moved(1)
    low = jnp.where(odd == 0, first, second)
    high = jnp.where(odd == 0, second, first)
    return jnp.concatenate([low, high], axis=1)


NEAR = (0, 2, 6, 4)
ODD = (1, 3, 7, 5)
STEP = 256
IN_VMEM = pl.BlockSpec(memory_space=pltpu.VMEM)
IN_SMEM = pl.BlockSpec(memory_space=pltpu.SMEM)
IN_PLACE = pl.BlockSpec(memory_space=pl.ANY)
WHOLE_VMEM = pltpu.CompilerParams(vmem_limit_bytes=62 << 20)


def columns_kept(rank, width):
    lane = lax.broadcasted_iota(jnp.int32, (1, width), 1)
    return (lane < rank).astype(jnp.bfloat16)


def solve_block(factor, known_rows, keep, i):
    block = jnp.dot(
        factor[pl.ds(STEP * i, STEP), : STEP * (i + 1)],
        known_rows,
        preferred_element_type=jnp.float32,
    )
    return block.astype(jnp.bfloat16) * keep


def column_kernel(ranks, here, there, factor, solved, values):
    order, across = solved.shape
    height = here.shape[1]
    pair = values.shape[0]
    width = across // pair
    col = lax.axis_index(COL)
    level = lax.axis_index("z")
    core = lax.axis_index("core")
    levels = lax.axis_size("z")
    for source, k in ((here, core), (there, 1 - core)):
        for n, shift in enumerate(NEAR + ODD):
            row = 2 * lax.rem(level + shift, levels) + k
            place = pl.ds(pl.multiple_of(height * row, height), height)
            factor[place, :] = source[n, :, :order]
            for u in range(pair):
                values[u, place, :] = source[n, :, order + width * u : order + width * (u + 1)]

    for u in range(pair):
        keep = columns_kept(ranks[col * pair + u], width)
        for i in range(order // STEP):
            solved[pl.ds(STEP * i, STEP), width * u : width * (u + 1)] = solve_block(
                factor, values[u, : STEP * (i + 1), :], keep, i
            )


def solve_columns(ranks, here, there, pair, width, order):
    return pl.pallas_call(
        column_kernel,
        out_shape=(
            jax.ShapeDtypeStruct((order, order), jnp.bfloat16),
            jax.ShapeDtypeStruct((order, pair * width), jnp.bfloat16),
        ),
        in_specs=[IN_SMEM, IN_VMEM, IN_VMEM],
        out_specs=(IN_VMEM, IN_VMEM),
        scratch_shapes=[pltpu.VMEM((pair, order, width), jnp.bfloat16)],
        compiler_params=pltpu.CompilerParams(vmem_limit_bytes=16 << 20),
        cost_estimate=pl.CostEstimate(
            flops=2 * order * order * width * pair, bytes_accessed=6 << 20, transcendentals=0
        ),
    )(ranks, here, there)


def row_kernel(
    ranks, factor_in, others_in, full, shares, core_blocks, factor, others, values, solved, sems
):
    cols, tiles, depth, width = full.shape
    order, across = others.shape
    row = lax.axis_index(ROW)
    col = lax.axis_index(COL)
    steps = order // STEP

    def factor_rows(i):
        block = pl.ds(STEP * i, STEP)
        return pltpu.make_async_copy(factor_in.at[block, :], factor.at[block, :], sems.at[i])

    def tile_values(t):
        return pltpu.make_async_copy(full.at[:, t], values.at[t], sems.at[steps + t])

    all_others = pltpu.make_async_copy(others_in, others, sems.at[steps + tiles])

    tile_values(0).start()
    for i in range(steps):
        factor_rows(i).start()
    all_others.start()
    for t in range(1, tiles):
        tile_values(t).start()

    def one(t, first):
        tile_values(t).wait()
        keep = columns_kept(ranks[row * tiles + t], width)
        for i in range(steps):
            if first:
                factor_rows(i).wait()
            known = STEP * (i + 1)
            solved[pl.ds(STEP * i, STEP), :] = solve_block(
                factor, values[t, : known // depth].reshape(known, width), keep, i
            )
        shares[t] = solved[pl.ds(pl.multiple_of(col * depth, depth), depth), :]
        if first:
            all_others.wait()
        paired = lax.dot_general(
            solved[...],
            others[...],
            (((0,), (0,)), ((), ())),
            preferred_element_type=jnp.float32,
        ).astype(jnp.bfloat16)
        for u in range(across // width):
            core_blocks[t, u] = paired[:, width * u : width * (u + 1)]

    def later(t, carry):
        one(t, False)
        return carry

    one(0, True)
    lax.fori_loop(1, tiles, later, 0)


def solve_rows(ranks, factor, others, full):
    cols, tiles, depth, width = full.shape
    order, across = others.shape
    return pl.pallas_call(
        row_kernel,
        out_shape=(
            jax.ShapeDtypeStruct((tiles, depth, width), jnp.bfloat16),
            jax.ShapeDtypeStruct((tiles, across // width, width, width), jnp.bfloat16),
        ),
        in_specs=[IN_SMEM, IN_PLACE, IN_PLACE, IN_PLACE],
        out_specs=(IN_VMEM, IN_VMEM),
        scratch_shapes=[
            pltpu.VMEM((order, order), jnp.bfloat16),
            pltpu.VMEM((order, across), jnp.bfloat16),
            pltpu.VMEM((tiles, cols, depth, width), jnp.bfloat16),
            pltpu.VMEM((order, width), jnp.bfloat16),
            pltpu.SemaphoreType.DMA((order // STEP + tiles + 1,)),
        ],
        compiler_params=WHOLE_VMEM,
        cost_estimate=pl.CostEstimate(
            flops=3 * order * order * width * tiles, bytes_accessed=6 << 20, transcendentals=0
        ),
    )(ranks, factor, others, full)


def from_level(value, shift):
    levels = lax.axis_size("z")
    return lax.ppermute(value, "z", [((z + shift) % levels, z) for z in range(levels)])


def per_device(panel, inverse_factor, ranks):
    tiles, depth, width = panel.shape
    col = lax.axis_index(COL)
    rows, cols = size_of(ROW), size_of(COL)
    pair = tiles * rows // cols
    order = cols * depth

    part = column_tiles(panel, col, rows, cols)
    factor = exchanged(copies_for(inverse_factor.T, COL), COL).reshape(order, -1).T
    packed = jnp.concatenate([factor, *part], axis=1)[None]

    copies, packed = lax.optimization_barrier((copies_for(panel, COL), packed))
    full = exchanged(copies, COL)
    opposite, above, below = from_level(packed, 4), from_level(packed, 2), from_level(packed, 6)
    upper = from_level(jnp.concatenate([packed, above]), 1)
    lower = from_level(jnp.concatenate([packed, below]), 7)
    here = jnp.concatenate([packed, above, below, opposite, upper, lower])
    there = lax.ppermute(here, "core", [(0, 1), (1, 0)])
    factor, others = solve_columns(ranks, here, there, pair, width, order)
    return solve_rows(ranks, factor, others, full)


def solution(mesh):
    split = Mesh(mesh.devices.reshape(8, 2, 4, 8), ALL)
    return jax.shard_map(
        per_device,
        mesh=split,
        in_specs=(P(ROW, COL, None), P(ROW, COL), P()),
        out_specs=(P(ROW, COL, None), P(ROW, COL, None, None)),
        check_vma=False,
    )
```

```python
import jax
import jax.numpy as jnp
from jax import lax
from jax.experimental import pallas as pl
from jax.experimental.pallas import tpu as pltpu
from jax.sharding import Mesh
from jax.sharding import PartitionSpec as P


ROW = ("z", "core")
COL = ("x", "y")
ALL = ROW + COL


def size_of(axes):
    axes = axes if isinstance(axes, tuple) else (axes,)
    count = 1
    for axis in axes:
        count *= lax.axis_size(axis)
    return count


def copies_for(value, axes):
    return jnp.broadcast_to(value, (size_of(axes), *value.shape))


def exchanged(copies, axes):
    return lax.all_to_all(copies, axes, split_axis=0, concat_axis=0, tiled=True)


def column_tiles(panel, col, rows, cols):
    odd = lax.rem(col, 2)
    pair = panel.shape[0] // 2

    def moved(flip):
        half = lax.bitwise_xor(odd, flip)
        part = lax.dynamic_slice_in_dim(panel, pair * half, pair, 0)
        pairs = [
            (r * cols + c, (c // 2) * cols + 2 * r + ((c % 2) ^ flip))
            for r in range(rows)
            for c in range(cols)
        ]
        return lax.ppermute(part, ALL, pairs)

    first, second = moved(0), moved(1)
    low = jnp.where(odd == 0, first, second)
    high = jnp.where(odd == 0, second, first)
    return jnp.concatenate([low, high], axis=1)


NEAR = (0, 2, 6, 4)
ODD = (1, 3, 7, 5)
STEP = 256
IN_VMEM = pl.BlockSpec(memory_space=pltpu.VMEM)
IN_SMEM = pl.BlockSpec(memory_space=pltpu.SMEM)
IN_PLACE = pl.BlockSpec(memory_space=pl.ANY)
WHOLE_VMEM = pltpu.CompilerParams(vmem_limit_bytes=62 << 20)


def columns_kept(rank, width):
    lane = lax.broadcasted_iota(jnp.int32, (1, width), 1)
    return (lane < rank).astype(jnp.bfloat16)


def solve_block(factor, known_rows, keep, i):
    block = jnp.dot(
        factor[pl.ds(STEP * i, STEP), : STEP * (i + 1)],
        known_rows,
        preferred_element_type=jnp.float32,
    )
    return block.astype(jnp.bfloat16) * keep


def column_kernel(ranks, near, near_core, odd, odd_core, factor, solved, values):
    order, across = solved.shape
    height = near.shape[1]
    pair = values.shape[0]
    width = across // pair
    steps = order // STEP
    col = lax.axis_index(COL)
    level = lax.axis_index("z")
    core = lax.axis_index("core")
    levels = lax.axis_size("z")
    for source, shifts, k in (
        (near, NEAR, core),
        (near_core, NEAR, 1 - core),
        (odd, ODD, core),
        (odd_core, ODD, 1 - core),
    ):
        for n, shift in enumerate(shifts):
            row = 2 * lax.rem(level + shift, levels) + k
            place = pl.ds(pl.multiple_of(height * row, height), height)
            factor[place, :] = source[n, :, :order]
            for u in range(pair):
                values[u, place, :] = source[n, :, order + width * u : order + width * (u + 1)]

    for u in range(pair):
        keep = columns_kept(ranks[col * pair + u], width)
        for i in range(steps):
            solved[pl.ds(STEP * i, STEP), width * u : width * (u + 1)] = solve_block(
                factor, values[u, : STEP * (i + 1), :], keep, i
            )


def solve_columns(ranks, near, near_core, odd, odd_core, pair, width, order):
    return pl.pallas_call(
        column_kernel,
        out_shape=(
            jax.ShapeDtypeStruct((order, order), jnp.bfloat16),
            jax.ShapeDtypeStruct((order, pair * width), jnp.bfloat16),
        ),
        in_specs=[IN_SMEM] + [IN_VMEM] * 4,
        out_specs=(IN_VMEM, IN_VMEM),
        scratch_shapes=[pltpu.VMEM((pair, order, width), jnp.bfloat16)],
        compiler_params=pltpu.CompilerParams(vmem_limit_bytes=16 << 20),
        cost_estimate=pl.CostEstimate(
            flops=2 * order * order * width * pair, bytes_accessed=6 << 20, transcendentals=0
        ),
    )(ranks, near, near_core, odd, odd_core)


def row_kernel(
    ranks, factor_in, others_in, full, shares, core_blocks, factor, others, values, solved, sems
):
    _, tiles, depth, width = full.shape
    order, across = others.shape
    row = lax.axis_index(ROW)
    col = lax.axis_index(COL)
    steps = order // STEP

    def factor_rows(i):
        block = pl.ds(STEP * i, STEP)
        return pltpu.make_async_copy(factor_in.at[block, :], factor.at[block, :], sems.at[i])

    def tile_values(t):
        return pltpu.make_async_copy(full.at[:, t], values.at[t], sems.at[steps + t])

    all_others = pltpu.make_async_copy(others_in, others, sems.at[steps + tiles])

    tile_values(0).start()
    for i in range(steps):
        factor_rows(i).start()
    all_others.start()
    for t in range(1, tiles):
        tile_values(t).start()

    def one(t, first):
        tile_values(t).wait()
        keep = columns_kept(ranks[row * tiles + t], width)
        for i in range(steps):
            if first:
                factor_rows(i).wait()
            known = STEP * (i + 1)
            solved[pl.ds(STEP * i, STEP), :] = solve_block(
                factor, values[t, : known // depth].reshape(known, width), keep, i
            )
        shares[t] = solved[pl.ds(pl.multiple_of(col * depth, depth), depth), :]
        if first:
            all_others.wait()
        paired = lax.dot_general(
            solved[...],
            others[...],
            (((0,), (0,)), ((), ())),
            preferred_element_type=jnp.float32,
        ).astype(jnp.bfloat16)
        for u in range(across // width):
            core_blocks[t, u] = paired[:, width * u : width * (u + 1)]

    def later(t, carry):
        one(t, False)
        return carry

    one(0, True)
    lax.fori_loop(1, tiles, later, 0)


def solve_rows(ranks, factor, others, full):
    cols, tiles, depth, width = full.shape
    order, across = others.shape
    return pl.pallas_call(
        row_kernel,
        out_shape=(
            jax.ShapeDtypeStruct((tiles, depth, width), jnp.bfloat16),
            jax.ShapeDtypeStruct((tiles, across // width, width, width), jnp.bfloat16),
        ),
        in_specs=[IN_SMEM, IN_PLACE, IN_PLACE, IN_PLACE],
        out_specs=(IN_VMEM, IN_VMEM),
        scratch_shapes=[
            pltpu.VMEM((order, order), jnp.bfloat16),
            pltpu.VMEM((order, across), jnp.bfloat16),
            pltpu.VMEM((tiles, cols, depth, width), jnp.bfloat16),
            pltpu.VMEM((order, width), jnp.bfloat16),
            pltpu.SemaphoreType.DMA((order // STEP + tiles + 1,)),
        ],
        compiler_params=WHOLE_VMEM,
        cost_estimate=pl.CostEstimate(
            flops=3 * order * order * width * tiles, bytes_accessed=6 << 20, transcendentals=0
        ),
    )(ranks, factor, others, full)


def from_level(value, shift):
    levels = lax.axis_size("z")
    return lax.ppermute(value, "z", [((z + shift) % levels, z) for z in range(levels)])


def other_core(value):
    return lax.ppermute(value, "core", [(0, 1), (1, 0)])


def per_device(panel, inverse_factor, ranks):
    tiles, depth, width = panel.shape
    col = lax.axis_index(COL)
    rows, cols = size_of(ROW), size_of(COL)
    pair = tiles * rows // cols
    order = cols * depth

    part = column_tiles(panel, col, rows, cols)
    factor = copies_for(inverse_factor.T, COL)
    factor = exchanged(factor, COL)
    factor = factor.reshape(order, -1).T
    packed = jnp.concatenate([factor, *part], axis=1)[None]

    copies = copies_for(panel, COL)
    copies, packed = lax.optimization_barrier((copies, packed))
    full = exchanged(copies, COL)
    opposite, above, below = from_level(packed, 4), from_level(packed, 2), from_level(packed, 6)
    near = jnp.concatenate([packed, above, below, opposite])
    upper, lower = jnp.concatenate([packed, above]), jnp.concatenate([packed, below])
    upper = from_level(upper, 1)
    lower = from_level(lower, 7)
    odd = jnp.concatenate([upper, lower])
    near_core = other_core(near)
    factor, others = solve_columns(
        ranks, near, near_core, odd, other_core(odd), pair, width, order
    )
    return solve_rows(ranks, factor, others, full)


def solution(mesh):
    split = Mesh(mesh.devices.reshape(8, 2, 4, 8), ALL)
    return jax.shard_map(
        per_device,
        mesh=split,
        in_specs=(P(ROW, COL, None), P(ROW, COL), P()),
        out_specs=(P(ROW, COL, None), P(ROW, COL, None, None)),
        check_vma=False,
    )
```

```python
import jax
import jax.numpy as jnp
from jax import lax
from jax.experimental import pallas as pl
from jax.experimental.pallas import tpu as pltpu
from jax.sharding import Mesh
from jax.sharding import PartitionSpec as P


ROW = ("z", "core")
COL = ("x", "y")
ALL = ROW + COL


def size_of(axes):
    axes = axes if isinstance(axes, tuple) else (axes,)
    count = 1
    for axis in axes:
        count *= lax.axis_size(axis)
    return count


def copies_for(value, axes):
    return jnp.broadcast_to(value, (size_of(axes), *value.shape))


def exchanged(copies, axes):
    return lax.all_to_all(copies, axes, split_axis=0, concat_axis=0, tiled=True)


def column_tiles(panel, col, rows, cols):
    odd = lax.rem(col, 2)
    pair = panel.shape[0] // 2
    moves = [
        (r * cols + c, (c // 2) * cols + 2 * r + c % 2) for r in range(rows) for c in range(cols)
    ]
    moved = lax.ppermute(panel, ALL, moves)
    kept = lax.dynamic_slice_in_dim(moved, pair * odd, pair, 0)
    given = lax.dynamic_slice_in_dim(moved, pair * (1 - odd), pair, 0)
    taken = lax.ppermute(given, "y", [(y, y ^ 1) for y in range(lax.axis_size("y"))])
    low = jnp.where(odd == 0, kept, taken)
    high = jnp.where(odd == 0, taken, kept)
    return jnp.concatenate([low, high], axis=1)


NEAR = (0, 2, 6, 4)
ODD = (1, 3, 7, 5)
STEP = 256
IN_VMEM = pl.BlockSpec(memory_space=pltpu.VMEM)
IN_SMEM = pl.BlockSpec(memory_space=pltpu.SMEM)
IN_PLACE = pl.BlockSpec(memory_space=pl.ANY)
WHOLE_VMEM = pltpu.CompilerParams(vmem_limit_bytes=62 << 20)


def columns_kept(rank, width):
    lane = lax.broadcasted_iota(jnp.int32, (1, width), 1)
    return (lane < rank).astype(jnp.bfloat16)


def solve_block(factor, known_rows, keep, i):
    block = jnp.dot(
        factor[pl.ds(STEP * i, STEP), : STEP * (i + 1)],
        known_rows,
        preferred_element_type=jnp.float32,
    )
    return block.astype(jnp.bfloat16) * keep


def column_kernel(ranks, near, near_core, odd, odd_core, factor, solved, values):
    order, across = solved.shape
    height = near.shape[1]
    pair = values.shape[0]
    width = across // pair
    steps = order // STEP
    col = lax.axis_index(COL)
    level = lax.axis_index("z")
    core = lax.axis_index("core")
    levels = lax.axis_size("z")
    for source, shifts, k in (
        (near, NEAR, core),
        (near_core, NEAR, 1 - core),
        (odd, ODD, core),
        (odd_core, ODD, 1 - core),
    ):
        for n, shift in enumerate(shifts):
            row = 2 * lax.rem(level + shift, levels) + k
            place = pl.ds(pl.multiple_of(height * row, height), height)
            factor[place, :] = source[n, :, :order]
            for u in range(pair):
                values[u, place, :] = source[n, :, order + width * u : order + width * (u + 1)]

    for u in range(pair):
        keep = columns_kept(ranks[col * pair + u], width)
        for i in range(steps):
            solved[pl.ds(STEP * i, STEP), width * u : width * (u + 1)] = solve_block(
                factor, values[u, : STEP * (i + 1), :], keep, i
            )


def solve_columns(ranks, near, near_core, odd, odd_core, pair, width, order):
    return pl.pallas_call(
        column_kernel,
        out_shape=(
            jax.ShapeDtypeStruct((order, order), jnp.bfloat16),
            jax.ShapeDtypeStruct((order, pair * width), jnp.bfloat16),
        ),
        in_specs=[IN_SMEM] + [IN_VMEM] * 4,
        out_specs=(IN_VMEM, IN_VMEM),
        scratch_shapes=[pltpu.VMEM((pair, order, width), jnp.bfloat16)],
        compiler_params=pltpu.CompilerParams(vmem_limit_bytes=16 << 20),
        cost_estimate=pl.CostEstimate(
            flops=2 * order * order * width * pair, bytes_accessed=6 << 20, transcendentals=0
        ),
    )(ranks, near, near_core, odd, odd_core)


def row_kernel(
    ranks, factor_in, others_in, full, shares, core_blocks, factor, others, values, solved, sems
):
    _, tiles, depth, width = full.shape
    order, across = others.shape
    row = lax.axis_index(ROW)
    col = lax.axis_index(COL)
    steps = order // STEP

    def factor_rows(i):
        block = pl.ds(STEP * i, STEP)
        return pltpu.make_async_copy(factor_in.at[block, :], factor.at[block, :], sems.at[i])

    def tile_values(t):
        return pltpu.make_async_copy(full.at[:, t], values.at[t], sems.at[steps + t])

    all_others = pltpu.make_async_copy(others_in, others, sems.at[steps + tiles])

    tile_values(0).start()
    for i in range(steps):
        factor_rows(i).start()
    all_others.start()
    for t in range(1, tiles):
        tile_values(t).start()

    def one(t, first):
        tile_values(t).wait()
        keep = columns_kept(ranks[row * tiles + t], width)
        for i in range(steps):
            if first:
                factor_rows(i).wait()
            known = STEP * (i + 1)
            solved[pl.ds(STEP * i, STEP), :] = solve_block(
                factor, values[t, : known // depth].reshape(known, width), keep, i
            )
        shares[t] = solved[pl.ds(pl.multiple_of(col * depth, depth), depth), :]
        if first:
            all_others.wait()
        paired = lax.dot_general(
            solved[...],
            others[...],
            (((0,), (0,)), ((), ())),
            preferred_element_type=jnp.float32,
        ).astype(jnp.bfloat16)
        for u in range(across // width):
            core_blocks[t, u] = paired[:, width * u : width * (u + 1)]

    def later(t, carry):
        one(t, False)
        return carry

    one(0, True)
    lax.fori_loop(1, tiles, later, 0)


def solve_rows(ranks, factor, others, full):
    cols, tiles, depth, width = full.shape
    order, across = others.shape
    return pl.pallas_call(
        row_kernel,
        out_shape=(
            jax.ShapeDtypeStruct((tiles, depth, width), jnp.bfloat16),
            jax.ShapeDtypeStruct((tiles, across // width, width, width), jnp.bfloat16),
        ),
        in_specs=[IN_SMEM, IN_PLACE, IN_PLACE, IN_PLACE],
        out_specs=(IN_VMEM, IN_VMEM),
        scratch_shapes=[
            pltpu.VMEM((order, order), jnp.bfloat16),
            pltpu.VMEM((order, across), jnp.bfloat16),
            pltpu.VMEM((tiles, cols, depth, width), jnp.bfloat16),
            pltpu.VMEM((order, width), jnp.bfloat16),
            pltpu.SemaphoreType.DMA((order // STEP + tiles + 1,)),
        ],
        compiler_params=WHOLE_VMEM,
        cost_estimate=pl.CostEstimate(
            flops=3 * order * order * width * tiles, bytes_accessed=6 << 20, transcendentals=0
        ),
    )(ranks, factor, others, full)


def from_level(value, shift):
    levels = lax.axis_size("z")
    return lax.ppermute(value, "z", [((z + shift) % levels, z) for z in range(levels)])


def other_core(value):
    return lax.ppermute(value, "core", [(0, 1), (1, 0)])


def per_device(panel, inverse_factor, ranks):
    tiles, depth, width = panel.shape
    col = lax.axis_index(COL)
    rows, cols = size_of(ROW), size_of(COL)
    pair = tiles * rows // cols
    order = cols * depth

    part = column_tiles(panel, col, rows, cols)
    factor = copies_for(inverse_factor.T, COL)
    factor = exchanged(factor, COL)
    factor = factor.reshape(order, -1).T
    packed = jnp.concatenate([factor, *part], axis=1)[None]

    copies = copies_for(panel, COL)
    copies, packed = lax.optimization_barrier((copies, packed))
    full = exchanged(copies, COL)
    above = from_level(packed, 2)
    below = from_level(packed, 6)
    opposite = from_level(packed, 4)
    near = jnp.concatenate([packed, above, below, opposite])
    upper, lower = jnp.concatenate([packed, above]), jnp.concatenate([packed, below])
    upper = from_level(upper, 1)
    lower = from_level(lower, 7)
    odd = jnp.concatenate([upper, lower])
    near_core = other_core(near)
    factor, others = solve_columns(
        ranks, near, near_core, odd, other_core(odd), pair, width, order
    )
    return solve_rows(ranks, factor, others, full)


def solution(mesh):
    split = Mesh(mesh.devices.reshape(8, 2, 4, 8), ALL)
    return jax.shard_map(
        per_device,
        mesh=split,
        in_specs=(P(ROW, COL, None), P(ROW, COL), P()),
        out_specs=(P(ROW, COL, None), P(ROW, COL, None, None)),
        check_vma=False,
    )
```

```python
import jax
import jax.numpy as jnp
from jax import lax
from jax.experimental import pallas as pl
from jax.experimental.pallas import tpu as pltpu
from jax.sharding import Mesh
from jax.sharding import PartitionSpec as P


ROW = ("z", "core")
COL = ("x", "y")
ALL = ROW + COL


def size_of(axes):
    axes = axes if isinstance(axes, tuple) else (axes,)
    count = 1
    for axis in axes:
        count *= lax.axis_size(axis)
    return count


def copies_for(value, axes):
    return jnp.broadcast_to(value, (size_of(axes), *value.shape))


def exchanged(copies, axes):
    return lax.all_to_all(copies, axes, split_axis=0, concat_axis=0, tiled=True)


def column_tiles(panel, col, rows, cols):
    odd = lax.rem(col, 2)
    pair = panel.shape[0] // 2
    moves = [
        (r * cols + c, (c // 2) * cols + 2 * r + c % 2) for r in range(rows) for c in range(cols)
    ]
    moved = lax.ppermute(panel, ALL, moves)
    kept = lax.dynamic_slice_in_dim(moved, pair * odd, pair, 0)
    given = lax.dynamic_slice_in_dim(moved, pair * (1 - odd), pair, 0)
    taken = lax.ppermute(given, "y", [(y, y ^ 1) for y in range(lax.axis_size("y"))])
    low = jnp.where(odd == 0, kept, taken)
    high = jnp.where(odd == 0, taken, kept)
    return jnp.concatenate([low, high], axis=1)


NEAR = (0, 2, 6, 4)
ODD = (1, 3, 7, 5)
STEP = 256
IN_VMEM = pl.BlockSpec(memory_space=pltpu.VMEM)
IN_SMEM = pl.BlockSpec(memory_space=pltpu.SMEM)
IN_PLACE = pl.BlockSpec(memory_space=pl.ANY)
WHOLE_VMEM = pltpu.CompilerParams(vmem_limit_bytes=62 << 20)


def columns_kept(rank, width):
    lane = lax.broadcasted_iota(jnp.int32, (1, width), 1)
    return (lane < rank).astype(jnp.bfloat16)


def solve_block(factor, known_rows, keep, i):
    block = jnp.dot(
        factor[pl.ds(STEP * i, STEP), : STEP * (i + 1)],
        known_rows,
        preferred_element_type=jnp.float32,
    )
    return block.astype(jnp.bfloat16) * keep


def column_kernel(ranks, near, near_core, odd, odd_core, factor, solved, values):
    order, across = solved.shape
    height = near.shape[1]
    pair = values.shape[0]
    width = across // pair
    steps = order // STEP
    col = lax.axis_index(COL)
    level = lax.axis_index("z")
    core = lax.axis_index("core")
    levels = lax.axis_size("z")
    for source, shifts, k in (
        (near, NEAR, core),
        (near_core, NEAR, 1 - core),
        (odd, ODD, core),
        (odd_core, ODD, 1 - core),
    ):
        for n, shift in enumerate(shifts):
            row = 2 * lax.rem(level + shift, levels) + k
            place = pl.ds(pl.multiple_of(height * row, height), height)
            factor[place, :] = source[n, :, :order]
            for u in range(pair):
                values[u, place, :] = source[n, :, order + width * u : order + width * (u + 1)]

    for u in range(pair):
        keep = columns_kept(ranks[col * pair + u], width)
        for i in range(steps):
            solved[pl.ds(STEP * i, STEP), width * u : width * (u + 1)] = solve_block(
                factor, values[u, : STEP * (i + 1), :], keep, i
            )


def solve_columns(ranks, near, near_core, odd, odd_core, pair, width, order):
    return pl.pallas_call(
        column_kernel,
        out_shape=(
            jax.ShapeDtypeStruct((order, order), jnp.bfloat16),
            jax.ShapeDtypeStruct((order, pair * width), jnp.bfloat16),
        ),
        in_specs=[IN_SMEM] + [IN_VMEM] * 4,
        out_specs=(IN_VMEM, IN_VMEM),
        scratch_shapes=[pltpu.VMEM((pair, order, width), jnp.bfloat16)],
        compiler_params=pltpu.CompilerParams(vmem_limit_bytes=16 << 20),
        cost_estimate=pl.CostEstimate(
            flops=2 * order * order * width * pair, bytes_accessed=6 << 20, transcendentals=0
        ),
    )(ranks, near, near_core, odd, odd_core)


def row_kernel(
    ranks, factor_in, others_in, full, shares, blocks_out, factor, others, values, solved, blocks, sems
):
    _, tiles, depth, width = full.shape
    order, across = others.shape
    row = lax.axis_index(ROW)
    col = lax.axis_index(COL)
    steps = order // STEP

    def factor_rows(i):
        block = pl.ds(STEP * i, STEP)
        return pltpu.make_async_copy(factor_in.at[block, :], factor.at[block, :], sems.at[i])

    def tile_values(t):
        return pltpu.make_async_copy(full.at[:, t], values.at[t], sems.at[steps + t])

    all_others = pltpu.make_async_copy(others_in, others, sems.at[steps + tiles])

    def tile_blocks(t):
        sem = sems.at[steps + tiles + 1 + t]
        return pltpu.make_async_copy(blocks.at[t], blocks_out.at[t], sem)

    tile_values(0).start()
    for i in range(steps):
        factor_rows(i).start()
    all_others.start()
    for t in range(1, tiles):
        tile_values(t).start()

    def one(t, first):
        tile_values(t).wait()
        keep = columns_kept(ranks[row * tiles + t], width)
        for i in range(steps):
            if first:
                factor_rows(i).wait()
            known = STEP * (i + 1)
            solved[pl.ds(STEP * i, STEP), :] = solve_block(
                factor, values[t, : known // depth].reshape(known, width), keep, i
            )
        shares[t] = solved[pl.ds(pl.multiple_of(col * depth, depth), depth), :]
        if first:
            all_others.wait()
        paired = lax.dot_general(
            solved[...],
            others[...],
            (((0,), (0,)), ((), ())),
            preferred_element_type=jnp.float32,
        ).astype(jnp.bfloat16)
        for u in range(across // width):
            blocks[t, u] = paired[:, width * u : width * (u + 1)]
        tile_blocks(t).start()

    def later(t, carry):
        one(t, False)
        return carry

    one(0, True)
    lax.fori_loop(1, tiles, later, 0)
    for t in range(tiles):
        tile_blocks(t).wait()


def solve_rows(ranks, factor, others, full):
    cols, tiles, depth, width = full.shape
    order, across = others.shape
    return pl.pallas_call(
        row_kernel,
        out_shape=(
            jax.ShapeDtypeStruct((tiles, depth, width), jnp.bfloat16),
            jax.ShapeDtypeStruct((tiles, across // width, width, width), jnp.bfloat16),
        ),
        in_specs=[IN_SMEM, IN_PLACE, IN_PLACE, IN_PLACE],
        out_specs=(IN_VMEM, IN_PLACE),
        scratch_shapes=[
            pltpu.VMEM((order, order), jnp.bfloat16),
            pltpu.VMEM((order, across), jnp.bfloat16),
            pltpu.VMEM((tiles, cols, depth, width), jnp.bfloat16),
            pltpu.VMEM((order, width), jnp.bfloat16),
            pltpu.VMEM((tiles, across // width, width, width), jnp.bfloat16),
            pltpu.SemaphoreType.DMA((order // STEP + 2 * tiles + 1,)),
        ],
        compiler_params=WHOLE_VMEM,
        cost_estimate=pl.CostEstimate(
            flops=3 * order * order * width * tiles, bytes_accessed=6 << 20, transcendentals=0
        ),
    )(ranks, factor, others, full)


def from_level(value, shift):
    levels = lax.axis_size("z")
    return lax.ppermute(value, "z", [((z + shift) % levels, z) for z in range(levels)])


def other_core(value):
    return lax.ppermute(value, "core", [(0, 1), (1, 0)])


def per_device(panel, inverse_factor, ranks):
    tiles, depth, width = panel.shape
    col = lax.axis_index(COL)
    rows, cols = size_of(ROW), size_of(COL)
    pair = tiles * rows // cols
    order = cols * depth

    part = column_tiles(panel, col, rows, cols)
    factor = copies_for(inverse_factor.T, COL)
    factor = exchanged(factor, COL)
    copies = copies_for(panel, COL)
    copies, factor = lax.optimization_barrier((copies, factor))
    packed = jnp.concatenate([factor.reshape(order, -1).T, *part], axis=1)[None]
    full = exchanged(copies, COL)
    above = from_level(packed, 2)
    below = from_level(packed, 6)
    opposite = from_level(packed, 4)
    near = jnp.concatenate([packed, above, below, opposite])
    upper, lower = jnp.concatenate([packed, above]), jnp.concatenate([packed, below])
    upper = from_level(upper, 1)
    lower = from_level(lower, 7)
    odd = jnp.concatenate([upper, lower])
    near_core = other_core(near)
    factor, others = solve_columns(
        ranks, near, near_core, odd, other_core(odd), pair, width, order
    )
    return solve_rows(ranks, factor, others, full)


def solution(mesh):
    split = Mesh(mesh.devices.reshape(8, 2, 4, 8), ALL)
    return jax.shard_map(
        per_device,
        mesh=split,
        in_specs=(P(ROW, COL, None), P(ROW, COL), P()),
        out_specs=(P(ROW, COL, None), P(ROW, COL, None, None)),
        check_vma=False,
    )
```

```python
import jax
import jax.numpy as jnp
from jax import lax
from jax.experimental import pallas as pl
from jax.experimental.pallas import tpu as pltpu
from jax.sharding import Mesh
from jax.sharding import PartitionSpec as P


ROW = ("z", "core")
COL = ("x", "y")
ALL = ROW + COL


def size_of(axes):
    axes = axes if isinstance(axes, tuple) else (axes,)
    count = 1
    for axis in axes:
        count *= lax.axis_size(axis)
    return count


def copies_for(value, axes):
    return jnp.broadcast_to(value, (size_of(axes), *value.shape))


def exchanged(copies, axes):
    return lax.all_to_all(copies, axes, split_axis=0, concat_axis=0, tiled=True)


def column_tiles(panel, col, rows, cols):
    odd = lax.rem(col, 2)
    pair = panel.shape[0] // 2
    moves = [
        (r * cols + c, (c // 2) * cols + 2 * r + c % 2) for r in range(rows) for c in range(cols)
    ]
    moved = lax.ppermute(panel, ALL, moves)
    kept = lax.dynamic_slice_in_dim(moved, pair * odd, pair, 0)
    given = lax.dynamic_slice_in_dim(moved, pair * (1 - odd), pair, 0)
    taken = lax.ppermute(given, "y", [(y, y ^ 1) for y in range(lax.axis_size("y"))])
    low = jnp.where(odd == 0, kept, taken)
    high = jnp.where(odd == 0, taken, kept)
    return jnp.concatenate([low, high], axis=1)


NEAR = (0, 2, 6, 4)
ODD = (1, 3, 7, 5)
STEP = 256
IN_VMEM = pl.BlockSpec(memory_space=pltpu.VMEM)
IN_SMEM = pl.BlockSpec(memory_space=pltpu.SMEM)
IN_PLACE = pl.BlockSpec(memory_space=pl.ANY)
WHOLE_VMEM = pltpu.CompilerParams(vmem_limit_bytes=62 << 20)


def columns_kept(rank, width):
    lane = lax.broadcasted_iota(jnp.int32, (1, width), 1)
    return (lane < rank).astype(jnp.bfloat16)


def solve_block(factor, known_rows, keep, i):
    block = jnp.dot(
        factor[pl.ds(STEP * i, STEP), : STEP * (i + 1)],
        known_rows,
        preferred_element_type=jnp.float32,
    )
    return block.astype(jnp.bfloat16) * keep


def column_kernel(ranks, near, near_core, odd, odd_core, factor, solved, values):
    order, across = solved.shape
    height = near.shape[1]
    pair = values.shape[0]
    width = across // pair
    steps = order // STEP
    col = lax.axis_index(COL)
    level = lax.axis_index("z")
    core = lax.axis_index("core")
    levels = lax.axis_size("z")
    for source, shifts, k in (
        (near, NEAR, core),
        (near_core, NEAR, 1 - core),
        (odd, ODD, core),
        (odd_core, ODD, 1 - core),
    ):
        for n, shift in enumerate(shifts):
            row = 2 * lax.rem(level + shift, levels) + k
            place = pl.ds(pl.multiple_of(height * row, height), height)
            factor[place, :] = source[n, :, :order]
            for u in range(pair):
                values[u, place, :] = source[n, :, order + width * u : order + width * (u + 1)]

    for u in range(pair):
        keep = columns_kept(ranks[col * pair + u], width)
        for i in range(steps):
            solved[pl.ds(STEP * i, STEP), width * u : width * (u + 1)] = solve_block(
                factor, values[u, : STEP * (i + 1), :], keep, i
            )


def solve_columns(ranks, near, near_core, odd, odd_core, pair, width, order):
    return pl.pallas_call(
        column_kernel,
        out_shape=(
            jax.ShapeDtypeStruct((order, order), jnp.bfloat16),
            jax.ShapeDtypeStruct((order, pair * width), jnp.bfloat16),
        ),
        in_specs=[IN_SMEM] + [IN_VMEM] * 4,
        out_specs=(IN_VMEM, IN_VMEM),
        scratch_shapes=[pltpu.VMEM((pair, order, width), jnp.bfloat16)],
        compiler_params=pltpu.CompilerParams(vmem_limit_bytes=16 << 20),
        cost_estimate=pl.CostEstimate(
            flops=2 * order * order * width * pair, bytes_accessed=6 << 20, transcendentals=0
        ),
    )(ranks, near, near_core, odd, odd_core)


def row_kernel(
    ranks, factor_in, others_in, full, shares, blocks_out, factor, others, values, solved, blocks, sems
):
    _, tiles, depth, width = full.shape
    order, across = others.shape
    row = lax.axis_index(ROW)
    col = lax.axis_index(COL)
    steps = order // STEP

    def factor_rows(i):
        block = pl.ds(STEP * i, STEP)
        return pltpu.make_async_copy(factor_in.at[block, :], factor.at[block, :], sems.at[i])

    def tile_values(t):
        return pltpu.make_async_copy(full.at[:, t], values.at[t], sems.at[steps + t])

    all_others = pltpu.make_async_copy(others_in, others, sems.at[steps + tiles])

    def tile_blocks(t):
        sem = sems.at[steps + tiles + 1 + t]
        return pltpu.make_async_copy(blocks.at[t], blocks_out.at[t], sem)

    tile_values(0).start()
    for i in range(steps):
        factor_rows(i).start()
    all_others.start()
    for t in range(1, tiles):
        tile_values(t).start()

    def one(t, first):
        tile_values(t).wait()
        keep = columns_kept(ranks[row * tiles + t], width)
        for i in range(steps):
            if first:
                factor_rows(i).wait()
            known = STEP * (i + 1)
            solved[pl.ds(STEP * i, STEP), :] = solve_block(
                factor, values[t, : known // depth].reshape(known, width), keep, i
            )
        shares[t] = solved[pl.ds(pl.multiple_of(col * depth, depth), depth), :]
        if first:
            all_others.wait()
        paired = lax.dot_general(
            solved[...],
            others[...],
            (((0,), (0,)), ((), ())),
            preferred_element_type=jnp.float32,
        ).astype(jnp.bfloat16)
        for u in range(across // width):
            blocks[t, u] = paired[:, width * u : width * (u + 1)]
        tile_blocks(t).start()

    def later(t, carry):
        one(t, False)
        return carry

    one(0, True)
    lax.fori_loop(1, tiles, later, 0)
    for t in range(tiles):
        tile_blocks(t).wait()


def solve_rows(ranks, factor, others, full):
    cols, tiles, depth, width = full.shape
    order, across = others.shape
    return pl.pallas_call(
        row_kernel,
        out_shape=(
            jax.ShapeDtypeStruct((tiles, depth, width), jnp.bfloat16),
            jax.ShapeDtypeStruct((tiles, across // width, width, width), jnp.bfloat16),
        ),
        in_specs=[IN_SMEM, IN_PLACE, IN_PLACE, IN_PLACE],
        out_specs=(IN_VMEM, IN_PLACE),
        scratch_shapes=[
            pltpu.VMEM((order, order), jnp.bfloat16),
            pltpu.VMEM((order, across), jnp.bfloat16),
            pltpu.VMEM((tiles, cols, depth, width), jnp.bfloat16),
            pltpu.VMEM((order, width), jnp.bfloat16),
            pltpu.VMEM((tiles, across // width, width, width), jnp.bfloat16),
            pltpu.SemaphoreType.DMA((order // STEP + 2 * tiles + 1,)),
        ],
        compiler_params=WHOLE_VMEM,
        cost_estimate=pl.CostEstimate(
            flops=3 * order * order * width * tiles, bytes_accessed=6 << 20, transcendentals=0
        ),
    )(ranks, factor, others, full)


def from_level(value, shift):
    levels = lax.axis_size("z")
    return lax.ppermute(value, "z", [((z + shift) % levels, z) for z in range(levels)])


def other_core(value):
    return lax.ppermute(value, "core", [(0, 1), (1, 0)])


def per_device(panel, inverse_factor, ranks):
    tiles, depth, width = panel.shape
    col = lax.axis_index(COL)
    rows, cols = size_of(ROW), size_of(COL)
    pair = tiles * rows // cols
    order = cols * depth

    part = column_tiles(panel, col, rows, cols)
    factor = copies_for(inverse_factor.T, COL)
    factor = exchanged(factor, COL)
    factor = factor.reshape(order, -1).T
    packed = jnp.concatenate([factor, *part], axis=1)[None]

    copies = copies_for(panel, COL)
    copies, packed = lax.optimization_barrier((copies, packed))
    full = exchanged(copies, COL)
    above = from_level(packed, 2)
    below = from_level(packed, 6)
    opposite = from_level(packed, 4)
    near = jnp.concatenate([packed, above, below, opposite])
    upper, lower = jnp.concatenate([packed, above]), jnp.concatenate([packed, below])
    upper = from_level(upper, 1)
    lower = from_level(lower, 7)
    odd = jnp.concatenate([upper, lower])
    near_core = other_core(near)
    factor, others = solve_columns(
        ranks, near, near_core, odd, other_core(odd), pair, width, order
    )
    return solve_rows(ranks, factor, others, full)


def solution(mesh):
    split = Mesh(mesh.devices.reshape(8, 2, 4, 8), ALL)
    return jax.shard_map(
        per_device,
        mesh=split,
        in_specs=(P(ROW, COL, None), P(ROW, COL), P()),
        out_specs=(P(ROW, COL, None), P(ROW, COL, None, None)),
        check_vma=False,
    )
```
